256 devices in a mesh: src: 64 (over z_hi, x, y, core), rcv: 4 (over z_lo).
Axes of the slice: x: 4, y: 4, z: 8 (z_hi: 2, z_lo: 4; z = z_hi * 4 + z_lo), core: 2. Of those that a mesh axis runs over, the one named last changes fastest.
Arguments:
- src_spec: bfloat16 [2, 16, 256, 4096], P(None, None, 'rcv', 'src'), may hold values from -6 to 6
- rcv_spec: bfloat16 [2, 16, 256, 1024], P(None, None, 'src', 'rcv'), may hold values from -6 to 6
- lag_table: int32 [16, 8192], replicated, may hold values from 0 to 511
- src_pos: int32 [4096], P('src'), may hold values from 0 to 8191
- rcv_pos: int32 [1024], P('rcv'), may hold values from 0 to 8191
Outputs:
- panel_src: float32 [16, 2, 4096, 256], P(None, None, ('src', 'rcv'))
- panel_rcv: float32 [16, 2, 256, 1024], P(None, None, 'src', 'rcv')
The draws below stay inside these ranges and needn't reach their ends.
All inputs are finite; a program needn't handle non-finite values.
Results may differ from the reference program's by a relative error of at most 0.0035.
Values may be sent and summed in bfloat16 or wider, within the bound.
A program may use at most 64 MiB of HBM per device.

```python
import math
import jax
import jax.numpy as jnp
from jax import lax

F = 256
P_SIZE = 16
WIN = 8
SEGS = 2
NPOS = 8192
NWIN = 16
S = 4096
R = 1024


def set_ends(array, own_key, smallest, top_value):
    place = [jax.random.randint(jax.random.fold_in(own_key, axis), (), 0, length) for axis, length in enumerate(array.shape)]
    main_axis = array.shape.index(max(array.shape))
    next_to = place[:main_axis] + [(place[main_axis] + 1) % array.shape[main_axis]] + place[main_axis + 1:]
    return array.at[tuple(place)].set(smallest).at[tuple(next_to)].set(top_value)


def shard_levels(rng, dims, cuts, least, largest):
    loudness, own = 1.0, jax.random.fold_in(rng, 6)
    for position, blocks in cuts:
        steps = jnp.exp(jax.random.uniform(jax.random.fold_in(own, position), (blocks,), jnp.float32, least / len(cuts), largest / len(cuts)))
        loudness = loudness * jnp.repeat(steps, dims[position] // blocks).reshape([-1 if axis == position else 1 for axis in range(len(dims))])
    return loudness


def normal_values(stream_key, extent, scale, reach, cuts=(), kind=jnp.bfloat16):
    values = scale * jax.random.normal(stream_key, extent, jnp.float32)
    if cuts:
        values = values * shard_levels(stream_key, extent, cuts, -0.22, 0.18)
    return jnp.clip(values, -reach, reach).astype(kind)


def setup_inputs(seed: int = 0) -> dict:
    seeds = jax.random.split(jax.random.key(seed), 6)
    return {
        "src_spec": normal_values(seeds[0], (2, NWIN, F, S), 1.0, 6.0, ((2, 4), (3, 64))),
        "rcv_spec": normal_values(seeds[1], (2, NWIN, F, R), 1.0, 6.0, ((2, 64), (3, 4))),
        "lag_table": set_ends(jax.random.randint(seeds[2], (P_SIZE, NPOS), 0, 2 * F), jax.random.fold_in(seeds[2], 1), 0, (2 * F) - 1).astype(jnp.int32),
        "src_pos": set_ends(jax.random.randint(seeds[3], (S,), 0, NPOS), jax.random.fold_in(seeds[3], 1), 0, NPOS - 1).astype(jnp.int32),
        "rcv_pos": set_ends(jax.random.randint(seeds[4], (R,), 0, NPOS), jax.random.fold_in(seeds[4], 1), 0, NPOS - 1).astype(jnp.int32),
    }


def product(left_op, right_op):
    return jnp.dot(left_op.astype(jnp.float32), right_op.astype(jnp.float32), precision=lax.Precision.HIGHEST, preferred_element_type=jnp.float32)

def phase_table(frequency, lags):
    index_mod = frequency * lags % (2 * F)
    angles = index_mod.astype(jnp.float32) * (math.pi / F)
    return (jnp.cos(angles), jnp.sin(angles))

def reference(src_spec, rcv_spec, lag_table, src_pos, rcv_pos):
    lag_src = jnp.take(lag_table, src_pos, axis=1)
    lag_rcv = jnp.take(lag_table, rcv_pos, axis=1)
    count_src = src_spec.shape[3]
    count_rcv = rcv_spec.shape[3]
    src_factor = 1.0 / math.sqrt(count_rcv)
    rcv_factor = 1.0 / math.sqrt(count_src)

    def per_freq(frequency):
        src_block = lax.dynamic_index_in_dim(src_spec, frequency, 2, keepdims=False).astype(jnp.float32)
        rcv_block = lax.dynamic_index_in_dim(rcv_spec, frequency, 2, keepdims=False).astype(jnp.float32)
        total_re = jnp.zeros((count_src, count_rcv), jnp.float32)
        total_im = jnp.zeros((count_src, count_rcv), jnp.float32)
        for segment in range(SEGS):
            src_re = src_block[0, segment * WIN:(segment + 1) * WIN]
            src_im = src_block[1, segment * WIN:(segment + 1) * WIN]
            rcv_re = rcv_block[0, segment * WIN:(segment + 1) * WIN]
            rcv_im = rcv_block[1, segment * WIN:(segment + 1) * WIN]
            real_part = product(src_re.T, rcv_re) + product(src_im.T, rcv_im)
            imag_part = product(src_im.T, rcv_re) - product(src_re.T, rcv_im)
            floor_mod = jnp.maximum(jnp.sqrt(real_part * real_part + imag_part * imag_part), 1.0)
            total_re = total_re + real_part / floor_mod
            total_im = total_im + imag_part / floor_mod
        stacked_re = (total_re / SEGS).astype(jnp.bfloat16)
        stacked_im = (total_im / SEGS).astype(jnp.bfloat16)
        rcv_cos, rcv_sin = phase_table(frequency, lag_rcv)
        src_cos, src_sin = phase_table(frequency, lag_src)
        rcv_cos_b = rcv_cos.astype(jnp.bfloat16)
        rcv_sin_b = rcv_sin.astype(jnp.bfloat16)
        src_cos_b = src_cos.astype(jnp.bfloat16)
        src_sin_b = src_sin.astype(jnp.bfloat16)
        sum_re = product(stacked_re, rcv_cos_b.T) - product(stacked_im, rcv_sin_b.T)
        sum_im = product(stacked_re, rcv_sin_b.T) + product(stacked_im, rcv_cos_b.T)
        panel_re = (sum_re * src_cos.T + sum_im * src_sin.T) * src_factor
        panel_im = (sum_im * src_cos.T - sum_re * src_sin.T) * src_factor
        other_re = product(stacked_re.T, src_cos_b.T) + product(stacked_im.T, src_sin_b.T)
        other_im = product(stacked_im.T, src_cos_b.T) - product(stacked_re.T, src_sin_b.T)
        rcvpan_re = (other_re * rcv_cos.T - other_im * rcv_sin.T) * rcv_factor
        rcvpan_im = (other_re * rcv_sin.T + other_im * rcv_cos.T) * rcv_factor
        return (jnp.stack([panel_re.T, panel_im.T], axis=1), jnp.stack([rcvpan_re.T, rcvpan_im.T], axis=1))
    src_all, rcv_all = lax.map(per_freq, jnp.arange(F, dtype=jnp.int32))
    return (jnp.transpose(src_all, (1, 2, 3, 0)), jnp.transpose(rcv_all, (1, 2, 0, 3)))
```

```python
import functools
import math

import jax
import jax.numpy as jnp
from jax import lax
from jax.experimental import pallas as pl
from jax.experimental.pallas import tpu as pltpu
from jax.sharding import PartitionSpec as P

MESH = pl.DeviceIdType.MESH
N_SRC = 64
N_RCV = 4
N_DEV = 256
N_FREQ = 256
N_SLOW = 16
N_S = 4096
N_R = 1024
SB = 64
RB = 256
TILE = 256
LAG_MID = 256


def lag_kernel(table_ref, pos_ref, src_ref, rcv_ref):
    n_pos = SB + RB
    n_hi = table_ref.shape[1] // 128
    pieces = [table_ref[:, h * 128:(h + 1) * 128] for h in range(n_hi)]
    table = jnp.concatenate(pieces, axis=0).astype(jnp.float32) - float(LAG_MID)
    pos = pos_ref[...]
    low = lax.rem(pos, 128)
    high = lax.div(pos, 128)
    pick = (lax.broadcasted_iota(jnp.int32, (128, n_pos), 0) == low).astype(jnp.float32)
    rows = jnp.dot(
        table.astype(jnp.bfloat16), pick.astype(jnp.bfloat16), preferred_element_type=jnp.float32
    )
    total = jnp.zeros((N_SLOW, n_pos), jnp.float32)
    for h in range(n_hi):
        total = total + jnp.where(high == h, rows[h * N_SLOW:(h + 1) * N_SLOW], 0.0)
    src = total[:, RB:RB + SB]
    src = jnp.concatenate([src[:8], src[8:]], axis=1)
    src_ref[...] = src.astype(jnp.bfloat16)
    rcv_ref[...] = total[:, :RB].astype(jnp.bfloat16)


def own_lags(lag_table, src_pos, rcv_pos):
    pos = jnp.concatenate([rcv_pos, src_pos])[None, :]
    return pl.pallas_call(
        lag_kernel,
        out_shape=(
            jax.ShapeDtypeStruct((8, 128), jnp.bfloat16),
            jax.ShapeDtypeStruct((N_SLOW, RB), jnp.bfloat16),
        ),
        name="own_lags",
    )(lag_table, pos)


def spread_kernel(s_ref, r_ref, so_ref, ro_ref, ssem, rsem, lsem, ssem2, rsem2, lsem2):
    i = lax.axis_index("src")
    j = lax.axis_index("rcv")
    own = lax.div(i, 16) == j
    away = jnp.logical_not(own)
    barrier = pltpu.get_barrier_semaphore()
    from_rcv = lax.div(i, 16)

    def greet(d, carry):
        peer = lax.rem(i + d, N_SRC)
        pl.semaphore_signal(barrier, inc=1, device_id=(peer, from_rcv), device_id_type=MESH)
        return carry

    lax.fori_loop(1, N_SRC, greet, 0)
    for d in range(1, N_RCV):
        pl.semaphore_signal(
            barrier, inc=1, device_id=(i, lax.rem(j + d, N_RCV)), device_id_type=MESH
        )

    @pl.when(away)
    def _():
        pl.semaphore_signal(barrier, inc=1, device_id=(i, from_rcv), device_id_type=MESH)
        pl.semaphore_wait(barrier, N_SRC + N_RCV - 1)

    @pl.when(own)
    def _():
        pl.semaphore_wait(barrier, N_SRC + N_RCV - 2)

    local = pltpu.make_async_copy(r_ref.at[j], ro_ref.at[j], lsem2)
    local.start()

    def send(d, carry):
        local_f = lax.rem(lax.rem(i, 16) * 4 + j + d, SB)
        dest_i = 16 * j + lax.div(local_f, 4)
        dest_j = lax.rem(local_f, 4)
        pltpu.make_async_remote_copy(
            s_ref.at[local_f], so_ref.at[i], ssem, rsem,
            device_id=(dest_i, dest_j), device_id_type=MESH,
        ).start()
        return carry

    for d in range(1, N_RCV):
        peer = lax.rem(j + d, N_RCV)
        pltpu.make_async_remote_copy(
            r_ref.at[peer], ro_ref.at[j], ssem2, rsem2, device_id=(i, peer), device_id_type=MESH
        ).start()
    lax.fori_loop(1, SB, send, 0)
    first = lax.rem(i, 16) * 4 + j
    whole = pltpu.make_async_remote_copy(
        s_ref, so_ref, ssem, rsem, device_id=(i, j), device_id_type=MESH
    )
    part = pltpu.make_async_remote_copy(
        s_ref.at[pl.ds(0, SB - 1)], so_ref.at[pl.ds(0, SB - 1)], ssem, rsem,
        device_id=(i, j), device_id_type=MESH,
    )

    @pl.when(own)
    def _():
        keep = pltpu.make_async_copy(s_ref.at[first], so_ref.at[i], lsem)
        keep.start()
        keep.wait()
        part.wait_send()
        part.wait_recv()

    @pl.when(away)
    def _():
        pltpu.make_async_remote_copy(
            s_ref.at[first], so_ref.at[i], ssem, rsem,
            device_id=(16 * j + lax.rem(i, 16), j), device_id_type=MESH,
        ).start()
        whole.wait_send()
        whole.wait_recv()

    local.wait()
    rest = pltpu.make_async_remote_copy(
        r_ref.at[pl.ds(0, N_RCV - 1)], ro_ref.at[pl.ds(0, N_RCV - 1)], ssem2, rsem2,
        device_id=(i, j), device_id_type=MESH,
    )
    rest.wait_send()
    rest.wait_recv()


def spread(src_pack, rcv_pack):
    return pl.pallas_call(
        spread_kernel,
        out_shape=(
            jax.ShapeDtypeStruct(src_pack.shape, src_pack.dtype),
            jax.ShapeDtypeStruct(rcv_pack.shape, rcv_pack.dtype),
        ),
        in_specs=[pl.BlockSpec(memory_space=pltpu.VMEM)] * 2,
        out_specs=(pl.BlockSpec(memory_space=pltpu.VMEM),) * 2,
        scratch_shapes=[pltpu.SemaphoreType.DMA] * 6,
        compiler_params=pltpu.CompilerParams(has_side_effects=True, collective_id=1),
        name="spread",
    )(src_pack, rcv_pack)


def unit_circle(m):
    quad = lax.shift_right_logical(m + 64, 7)
    x = (m - quad * 128).astype(jnp.float32) * (math.pi / N_FREQ)
    x2 = x * x
    sin = x * (1.0 + x2 * (-1 / 6 + x2 * (1 / 120 + x2 * (-1 / 5040 + x2 * (1 / 362880)))))
    cos = 1.0 + x2 * (-0.5 + x2 * (1 / 24 + x2 * (-1 / 720 + x2 * (1 / 40320))))
    odd = (quad & 1) == 1
    base_cos = jnp.where(odd, sin, cos)
    base_sin = jnp.where(odd, cos, sin)
    turn = quad & 3
    cos_out = jnp.where((turn == 1) | (turn == 2), -base_cos, base_cos)
    sin_out = jnp.where(turn >= 2, -base_sin, base_sin)
    return cos_out, sin_out


def phases(lag, freq):
    m = ((lag + float(LAG_MID)).astype(jnp.int32) * freq) & (2 * N_FREQ - 1)
    return unit_circle(m)


def cross_kernel(
    freq_ref, s_ref, r_ref, ms_ref, mr_ref,
    left_ref, er_ref, w_ref, es_ref, g_ref, acc_ref, turn_ref,
):
    freq = freq_ref[0]
    bf = jnp.bfloat16
    f32 = jnp.float32
    rcv = jnp.concatenate([r_ref[q, :32] for q in range(N_RCV)], axis=1).astype(f32)
    swapped = jnp.concatenate([-rcv[16:], rcv[:16]], axis=0)
    seg = (lax.broadcasted_iota(jnp.int32, rcv.shape, 0) & 15) < 8
    stack = jnp.concatenate(
        [
            jnp.where(seg, rcv, 0.0),
            jnp.where(seg, swapped, 0.0),
            jnp.where(seg, 0.0, rcv),
            jnp.where(seg, 0.0, swapped),
        ],
        axis=0,
    )
    turned = jnp.transpose(stack)
    block = lax.broadcasted_iota(jnp.int32, turned.shape, 1) // 32
    for v in range(4):
        left_ref[v] = jnp.where(block == v, turned, 0.0).astype(bf)
    lag_r = jnp.concatenate([r_ref[q, 32:48] for q in range(N_RCV)], axis=1).astype(f32)
    cos_r, sin_r = phases(lag_r, freq)
    er_ref[0] = jnp.concatenate([cos_r, sin_r], axis=0)
    er_ref[1] = jnp.concatenate([-sin_r, cos_r], axis=0)
    lane = lax.broadcasted_iota(jnp.int32, (24, 128), 1) < 64

    acc_ref[...] = jnp.zeros_like(acc_ref)

    def step(t, carry):
        parts = []
        for pair in range(2):
            a = s_ref[4 * t + 2 * pair].astype(f32)
            b = s_ref[4 * t + 2 * pair + 1].astype(f32)
            low = jnp.where(lane, a, pltpu.roll(b, 64, 1))
            high = jnp.where(lane, pltpu.roll(a, 64, 1), b)
            parts.append((low, high))
        low = jnp.concatenate([parts[0][0], parts[1][0]], axis=1)
        high = jnp.concatenate([parts[0][1], parts[1][1]], axis=1)
        weights = jnp.concatenate([low[:16], high[:16]], axis=0).astype(bf)
        weights = jnp.concatenate([weights] * 4, axis=0)
        lag_s = jnp.concatenate([low[16:], high[16:]], axis=0)
        cos_s, sin_s = phases(lag_s, freq)
        for q in range(4):
            rows = slice(q * 256, (q + 1) * 256)
            re0 = jnp.dot(left_ref[0, rows], weights, preferred_element_type=f32)
            im0 = jnp.dot(left_ref[1, rows], weights, preferred_element_type=f32)
            re1 = jnp.dot(left_ref[2, rows], weights, preferred_element_type=f32)
            im1 = jnp.dot(left_ref[3, rows], weights, preferred_element_type=f32)
            inv0 = lax.rsqrt(jnp.maximum(re0 * re0 + im0 * im0, 1.0))
            inv1 = lax.rsqrt(jnp.maximum(re1 * re1 + im1 * im1, 1.0))
            g_ref[0, rows] = (re0 * inv0 + re1 * inv1).astype(bf)
            g_ref[1, rows] = (im0 * inv0 + im1 * inv1).astype(bf)
        sums = jnp.dot(er_ref[0].astype(bf), g_ref[0], preferred_element_type=f32)
        sums = sums + jnp.dot(er_ref[1].astype(bf), g_ref[1], preferred_element_type=f32)
        cos_b = cos_s.astype(bf)
        sin_b = sin_s.astype(bf)
        es0 = jnp.concatenate([cos_b, -sin_b], axis=0)
        es1 = jnp.concatenate([sin_b, cos_b], axis=0)
        nt = (((1,), (1,)), ((), ()))
        acc_ref[...] += lax.dot_general(
            es0, g_ref[0], nt, preferred_element_type=f32
        ) + lax.dot_general(es1, g_ref[1], nt, preferred_element_type=f32)
        factor = 0.5 / math.sqrt(N_R)
        sum_re, sum_im = sums[:16], sums[16:]
        out_re = (sum_re * cos_s + sum_im * sin_s) * factor
        out_im = (sum_im * cos_s - sum_re * sin_s) * factor
        both = jnp.concatenate([out_re, out_im], axis=0)
        wide = jnp.concatenate([both] * 4, axis=0)
        turn_ref[...] = jnp.transpose(wide).reshape(16, 16, 128)
        part = lax.broadcasted_iota(jnp.int32, (16, 4, 128), 2) // 32
        msg = jnp.where(
            part < 2,
            jnp.where(part == 0, turn_ref[:, 0:4], turn_ref[:, 4:8]),
            jnp.where(part == 2, turn_ref[:, 8:12], turn_ref[:, 12:16]),
        )
        ms_ref[pl.ds(t * 16, 16)] = msg.astype(bf)
        return carry

    lax.fori_loop(0, N_S // TILE, step, 0)
    factor = 0.5 / math.sqrt(N_S)
    acc_re, acc_im = acc_ref[:16], acc_ref[16:]
    out_re = (acc_re * cos_r - acc_im * sin_r) * factor
    out_im = (acc_re * sin_r + acc_im * cos_r) * factor
    both = jnp.concatenate([out_re, out_im], axis=0).astype(bf)
    for q in range(N_RCV):
        mr_ref[q] = both[:, q * RB:(q + 1) * RB]


def cross(freq, src_all, rcv_all):
    return pl.pallas_call(
        cross_kernel,
        out_shape=(
            jax.ShapeDtypeStruct((N_DEV, 4, 128), jnp.bfloat16),
            jax.ShapeDtypeStruct((N_RCV, 2 * N_SLOW, RB), jnp.bfloat16),
        ),
        in_specs=[
            pl.BlockSpec(memory_space=pltpu.SMEM),
            pl.BlockSpec(memory_space=pltpu.VMEM),
            pl.BlockSpec(memory_space=pltpu.VMEM),
        ],
        out_specs=(pl.BlockSpec(memory_space=pltpu.VMEM),) * 2,
        scratch_shapes=[
            pltpu.VMEM((4, N_R, 128), jnp.bfloat16),
            pltpu.VMEM((2, 2 * N_SLOW, N_R), jnp.float32),
            pltpu.VMEM((128, TILE), jnp.bfloat16),
            pltpu.VMEM((2, 2 * N_SLOW, TILE), jnp.float32),
            pltpu.VMEM((2, N_R, TILE), jnp.bfloat16),
            pltpu.VMEM((2 * N_SLOW, N_R), jnp.float32),
            pltpu.VMEM((16, 16, 128), jnp.float32),
        ],
        name="cross",
    )(freq, src_all, rcv_all)


def collect_kernel(s_ref, r_ref, so_ref, ro_ref, ssem, rsem, lsem, ssem2, rsem2, lsem2):
    i = lax.axis_index("src")
    j = lax.axis_index("rcv")
    me = i * N_RCV + j
    keep = pltpu.make_async_copy(s_ref.at[me], so_ref.at[me], lsem)
    keep2 = pltpu.make_async_copy(r_ref.at[j], ro_ref.at[j], lsem2)
    keep.start()
    keep2.start()
    barrier = pltpu.get_barrier_semaphore()

    def greet(d, carry):
        peer = lax.rem(me + d, N_DEV)
        pl.semaphore_signal(
            barrier, inc=1, device_id=(lax.div(peer, N_RCV), lax.rem(peer, N_RCV)),
            device_id_type=MESH,
        )
        return carry

    lax.fori_loop(1, N_DEV, greet, 0)
    pl.semaphore_wait(barrier, N_DEV - 1)
    for d in range(1, N_RCV):
        peer = lax.rem(j + d, N_RCV)
        pltpu.make_async_remote_copy(
            r_ref.at[peer], ro_ref.at[j], ssem2, rsem2, device_id=(i, peer), device_id_type=MESH
        ).start()

    def send(d, carry):
        peer = lax.rem(me + d, N_DEV)
        pltpu.make_async_remote_copy(
            s_ref.at[peer], so_ref.at[me], ssem, rsem,
            device_id=(lax.div(peer, N_RCV), lax.rem(peer, N_RCV)), device_id_type=MESH,
        ).start()
        return carry

    lax.fori_loop(1, N_DEV, send, 0)
    keep.wait()
    keep2.wait()
    rest2 = pltpu.make_async_remote_copy(
        r_ref.at[pl.ds(0, N_RCV - 1)], ro_ref.at[pl.ds(0, N_RCV - 1)], ssem2, rsem2,
        device_id=(i, j), device_id_type=MESH,
    )
    rest = pltpu.make_async_remote_copy(
        s_ref.at[pl.ds(0, N_DEV - 1)], so_ref.at[pl.ds(0, N_DEV - 1)], ssem, rsem,
        device_id=(i, j), device_id_type=MESH,
    )
    rest2.wait_send()
    rest2.wait_recv()
    rest.wait_send()
    rest.wait_recv()


def collect(src_msg, rcv_msg):
    return pl.pallas_call(
        collect_kernel,
        out_shape=(
            jax.ShapeDtypeStruct(src_msg.shape, src_msg.dtype),
            jax.ShapeDtypeStruct(rcv_msg.shape, rcv_msg.dtype),
        ),
        in_specs=[pl.BlockSpec(memory_space=pltpu.VMEM)] * 2,
        out_specs=(pl.BlockSpec(memory_space=pltpu.VMEM),) * 2,
        scratch_shapes=[pltpu.SemaphoreType.DMA] * 6,
        compiler_params=pltpu.CompilerParams(has_side_effects=True, collective_id=2),
        name="collect",
    )(src_msg, rcv_msg)


def arrange_kernel(m_ref, o_ref):
    q = lax.broadcasted_iota(jnp.int32, (512, 128), 0)
    k = lax.broadcasted_iota(jnp.int32, (512, 128), 1)
    p, c, s = q // 32, (q // 16) & 1, q & 15
    lane = (s // 4) * 32 + c * 16 + p
    total = jnp.zeros((512, N_FREQ), jnp.float32)
    nt = (((1,), (1,)), ((), ()))
    for row in range(4):
        pick = jnp.where((k == lane) & ((s & 3) == row), 1.0, 0.0).astype(jnp.bfloat16)
        total = total + lax.dot_general(
            pick, m_ref[:, row, :], nt, preferred_element_type=jnp.float32
        )
    o_ref[...] = total


def arrange(msg):
    return pl.pallas_call(
        arrange_kernel,
        out_shape=jax.ShapeDtypeStruct((512, N_FREQ), jnp.float32),
        name="arrange",
    )(msg)


def per_device(src_spec, rcv_spec, lag_table, src_pos, rcv_pos):
    lag_s, lag_r = own_lags(lag_table, src_pos, rcv_pos)
    src_rows = jnp.transpose(src_spec, (2, 1, 0, 3)).reshape(SB, 16, 128)
    src_pack = jnp.concatenate([src_rows, jnp.broadcast_to(lag_s, (SB, 8, 128))], axis=1)
    rcv_rows = jnp.transpose(rcv_spec, (2, 0, 1, 3)).reshape(N_RCV, 32, RB)
    rcv_pack = jnp.concatenate([rcv_rows, jnp.broadcast_to(lag_r, (N_RCV, 16, RB))], axis=1)
    src_all, rcv_all = spread(src_pack, rcv_pack)
    freq = (lax.axis_index("src") * N_RCV + lax.axis_index("rcv")).astype(jnp.int32).reshape(1)
    src_msg, rcv_msg = cross(freq, src_all, rcv_all)
    src_got, rcv_got = collect(src_msg, rcv_msg)
    panel_src = arrange(src_got).reshape(N_SLOW, 2, 16, N_FREQ)
    rcv_got = rcv_got.reshape(N_RCV, 2, N_SLOW, RB)
    panel_rcv = jnp.transpose(rcv_got, (2, 1, 0, 3)).astype(jnp.float32)
    return (panel_src, panel_rcv)


def solution(mesh):
    placed = (P(None, None, "rcv", "src"), P(None, None, "src", "rcv"), P(), P("src"), P("rcv"))
    return jax.shard_map(
        per_device,
        mesh=mesh,
        in_specs=placed,
        out_specs=(P(None, None, ("src", "rcv"), None), P(None, None, "src", "rcv")),
        check_vma=False,
    )
```

```python
import functools
import math

import jax
import jax.numpy as jnp
from jax import lax
from jax.experimental import pallas as pl
from jax.experimental.pallas import tpu as pltpu
from jax.sharding import PartitionSpec as P

MESH = pl.DeviceIdType.MESH
N_SRC = 64
N_RCV = 4
N_DEV = 256
N_FREQ = 256
N_SLOW = 16
N_S = 4096
N_R = 1024
SB = 64
RB = 256
TILE = 256
LAG_MID = 256


def own_lags(table_ref, pos_ref):
    n_pos = SB + RB
    n_hi = table_ref.shape[1] // 128
    pieces = [table_ref[:, h * 128:(h + 1) * 128] for h in range(n_hi)]
    table = jnp.concatenate(pieces, axis=0).astype(jnp.float32) - float(LAG_MID)
    pos = pos_ref[...]
    low = pos & 127
    high = lax.shift_right_logical(pos, 7)
    pick = (lax.broadcasted_iota(jnp.int32, (128, n_pos), 0) == low).astype(jnp.float32)
    rows = jnp.dot(
        table.astype(jnp.bfloat16), pick.astype(jnp.bfloat16), preferred_element_type=jnp.float32
    )
    total = jnp.zeros((N_SLOW, n_pos), jnp.float32)
    for h in range(n_hi):
        total = total + jnp.where(high == h, rows[h * N_SLOW:(h + 1) * N_SLOW], 0.0)
    src = total[:, RB:RB + SB]
    src = jnp.concatenate([src[:8], src[8:]], axis=1)
    return src.astype(jnp.bfloat16), total[:, :RB].astype(jnp.bfloat16)


def unit_circle(m):
    quad = lax.shift_right_logical(m + 64, 7)
    x = (m - quad * 128).astype(jnp.float32) * (math.pi / N_FREQ)
    x2 = x * x
    sin = x * (1.0 + x2 * (-1 / 6 + x2 * (1 / 120 + x2 * (-1 / 5040 + x2 * (1 / 362880)))))
    cos = 1.0 + x2 * (-0.5 + x2 * (1 / 24 + x2 * (-1 / 720 + x2 * (1 / 40320))))
    odd = (quad & 1) == 1
    base_cos = jnp.where(odd, sin, cos)
    base_sin = jnp.where(odd, cos, sin)
    turn = quad & 3
    cos_out = jnp.where((turn == 1) | (turn == 2), -base_cos, base_cos)
    sin_out = jnp.where(turn >= 2, -base_sin, base_sin)
    return cos_out, sin_out


def phases(lag, freq):
    m = ((lag + float(LAG_MID)).astype(jnp.int32) * freq) & (2 * N_FREQ - 1)
    return unit_circle(m)


def prepare_receivers(r_ref, left_ref, er_ref, freq):
    bf = jnp.bfloat16
    f32 = jnp.float32
    rcv = jnp.concatenate([r_ref[q, :32] for q in range(N_RCV)], axis=1).astype(f32)
    swapped = jnp.concatenate([-rcv[16:], rcv[:16]], axis=0)
    seg = (lax.broadcasted_iota(jnp.int32, rcv.shape, 0) & 15) < 8
    variants = [
        jnp.where(seg, rcv, 0.0),
        jnp.where(seg, swapped, 0.0),
        jnp.where(seg, 0.0, rcv),
        jnp.where(seg, 0.0, swapped),
    ]
    turned = jnp.transpose(jnp.concatenate(variants, axis=0))
    for v in range(4):
        left_ref[:, v] = turned[:, 32 * v:32 * v + 32].reshape(N_R // 16, 16, 32).astype(bf)
    lag_r = jnp.concatenate([r_ref[q, 32:48] for q in range(N_RCV)], axis=1).astype(f32)
    cos_r, sin_r = phases(lag_r, freq)
    upper = jnp.concatenate([cos_r, sin_r], axis=0).astype(bf)
    lower = jnp.concatenate([-sin_r, cos_r], axis=0).astype(bf)
    for q in range(4):
        cols = slice(q * RB, (q + 1) * RB)
        er_ref[q] = jnp.concatenate([upper[:, cols], lower[:, cols]], axis=1)
    return cos_r, sin_r


def prepare_sources(s_ref, w_ref, ph_ref, freq):
    f32 = jnp.float32
    lane = lax.broadcasted_iota(jnp.int32, (24, 128), 1) < 64

    def prep(t, carry):
        parts = []
        for pair in range(2):
            a = s_ref[4 * t + 2 * pair].astype(f32)
            b = s_ref[4 * t + 2 * pair + 1].astype(f32)
            low = jnp.where(lane, a, pltpu.roll(b, 64, 1))
            high = jnp.where(lane, pltpu.roll(a, 64, 1), b)
            parts.append((low, high))
        low = jnp.concatenate([parts[0][0], parts[1][0]], axis=1)
        high = jnp.concatenate([parts[0][1], parts[1][1]], axis=1)
        w_ref[t] = jnp.concatenate([low[:16], high[:16]], axis=0).astype(jnp.bfloat16)
        lag_s = jnp.concatenate([low[16:], high[16:]], axis=0)
        cos_s, sin_s = phases(lag_s, freq)
        ph_ref[t] = jnp.concatenate([cos_s, sin_s], axis=0)
        return carry

    lax.fori_loop(0, N_S // TILE, prep, 0)


def cross_chunk(left_ref, weights, g_ref, q):
    f32 = jnp.float32
    bf = jnp.bfloat16
    halves = []
    for h in range(2):
        lhs = left_ref[q * 16 + 8 * h:q * 16 + 8 * h + 8].reshape(512, 32)
        halves.append(jnp.dot(lhs, weights, preferred_element_type=f32))
    for k in range(16):
        h, base = k % 2, (k // 2) * 64
        re0, im0, re1, im1 = [halves[h][base + v * 16:base + v * 16 + 16] for v in range(4)]
        inv0 = lax.rsqrt(jnp.maximum(re0 * re0 + im0 * im0, 1.0))
        inv1 = lax.rsqrt(jnp.maximum(re1 * re1 + im1 * im1, 1.0))
        row = 128 * h + 16 * (k // 2)
        g_ref[row:row + 16] = (re0 * inv0 + re1 * inv1).astype(bf)
        g_ref[RB + row:RB + row + 16] = (im0 * inv0 + im1 * inv1).astype(bf)


def slant_chunk(er_ref, es0, es1, g_ref, acc_ref, q):
    f32 = jnp.float32
    nt = (((1,), (1,)), ((), ()))
    cols = slice(q * RB, (q + 1) * RB)
    acc_ref[:, cols] += lax.dot_general(
        es0, g_ref[:RB], nt, preferred_element_type=f32
    ) + lax.dot_general(es1, g_ref[RB:], nt, preferred_element_type=f32)
    return jnp.dot(er_ref[q], g_ref[...], preferred_element_type=f32)


def message(sums, phase, turn_ref):
    factor = 0.5 / math.sqrt(N_R)
    cos_s, sin_s = phase[:16], phase[16:]
    sum_re, sum_im = sums[:16], sums[16:]
    out_re = (sum_re * cos_s + sum_im * sin_s) * factor
    out_im = (sum_im * cos_s - sum_re * sin_s) * factor
    both = jnp.concatenate([out_re, out_im], axis=0)
    wide = jnp.concatenate([both] * 4, axis=0)
    turn_ref[...] = jnp.transpose(wide).reshape(16, 16, 128)
    part = lax.broadcasted_iota(jnp.int32, (16, 4, 128), 2) // 32
    msg = jnp.where(
        part < 2,
        jnp.where(part == 0, turn_ref[:, 0:4], turn_ref[:, 4:8]),
        jnp.where(part == 2, turn_ref[:, 8:12], turn_ref[:, 12:16]),
    )
    return msg.astype(jnp.bfloat16)


def remote(src, dst, send_sem, recv_sem, dest):
    return pltpu.make_async_remote_copy(
        src, dst, send_sem, recv_sem, device_id=dest, device_id_type=MESH
    )


def panels_kernel(
    s_ref, r_ref, table_ref, pos_ref, so_ref, ro_ref,
    sp_ref, rp_ref, sa_ref, ra_ref, ms_ref, mr_ref,
    left_ref, er_ref, w_ref, ph_ref, g0_ref, g1_ref, g2_ref, g3_ref, sums_ref, acc_ref, turn_ref,
    in_send, in_recv, in_keep, rin_send, rin_recv, rin_keep,
    out_send, out_recv, out_keep, rout_send, rout_recv, rout_keep, ready,
):
    bf = jnp.bfloat16
    f32 = jnp.float32
    i = lax.axis_index("src")
    j = lax.axis_index("rcv")
    me = i * N_RCV + j
    freq = me
    g_refs = (g0_ref, g1_ref, g2_ref, g3_ref)
    n_tiles = N_S // TILE
    barrier = pltpu.get_barrier_semaphore()
    block = lax.div(i, 16)
    own = block == j
    away = jnp.logical_not(own)

    def greet(d, carry):
        pl.semaphore_signal(
            barrier, inc=1, device_id=(lax.rem(i + d, N_SRC), block), device_id_type=MESH
        )
        return carry

    lax.fori_loop(1, N_SRC, greet, 0)
    for d in range(1, N_RCV):
        pl.semaphore_signal(
            barrier, inc=1, device_id=(i, lax.rem(j + d, N_RCV)), device_id_type=MESH
        )

    @pl.when(away)
    def _():
        pl.semaphore_signal(barrier, inc=1, device_id=(i, block), device_id_type=MESH)

    lag_s, lag_r = own_lags(table_ref, pos_ref)
    sp_ref[:, :16] = s_ref[...]
    sp_ref[:, 16:] = jnp.broadcast_to(lag_s[None], (SB, 8, 128))
    rp_ref[:, :32] = r_ref[...]
    rp_ref[:, 32:] = jnp.broadcast_to(lag_r[None], (N_RCV, N_SLOW, RB))

    @pl.when(away)
    def _():
        pl.semaphore_wait(barrier, N_SRC + N_RCV - 1)

    @pl.when(own)
    def _():
        pl.semaphore_wait(barrier, N_SRC + N_RCV - 2)

    for d in range(1, N_RCV):
        pl.semaphore_signal(
            ready, inc=1, device_id=(i, lax.rem(j + d, N_RCV)), device_id_type=MESH
        )

    rin_local = pltpu.make_async_copy(rp_ref.at[j], ra_ref.at[j], rin_keep)
    rin_local.start()
    for d in range(1, N_RCV):
        peer = lax.rem(j + d, N_RCV)
        remote(rp_ref.at[peer], ra_ref.at[j], rin_send, rin_recv, (i, peer)).start()

    def send_in(d, carry):
        local_f = lax.rem(lax.rem(i, 16) * 4 + j + d, SB)
        dest = (16 * j + lax.div(local_f, 4), lax.rem(local_f, 4))
        remote(sp_ref.at[local_f], sa_ref.at[i], in_send, in_recv, dest).start()
        return carry

    lax.fori_loop(1, SB, send_in, 0)
    first_f = lax.rem(i, 16) * 4 + j

    @pl.when(own)
    def _():
        pltpu.make_async_copy(sp_ref.at[first_f], sa_ref.at[i], in_keep).start()

    @pl.when(away)
    def _():
        remote(
            sp_ref.at[first_f], sa_ref.at[i], in_send, in_recv, (16 * j + lax.rem(i, 16), j)
        ).start()

    acc_ref[...] = jnp.zeros_like(acc_ref)
    sums_ref[...] = jnp.zeros_like(sums_ref)
    g3_ref[...] = jnp.zeros_like(g3_ref)
    rin_local.wait()
    rin_rest = remote(
        rp_ref.at[pl.ds(0, N_RCV - 1)], ra_ref.at[pl.ds(0, N_RCV - 1)], rin_send, rin_recv, (i, j)
    )
    rin_rest.wait_send()
    rin_rest.wait_recv()
    cos_r, sin_r = prepare_receivers(ra_ref, left_ref, er_ref, freq)

    @pl.when(own)
    def _():
        pltpu.make_async_copy(sp_ref.at[first_f], sa_ref.at[i], in_keep).wait()
        part = remote(
            sp_ref.at[pl.ds(0, SB - 1)], sa_ref.at[pl.ds(0, SB - 1)], in_send, in_recv, (i, j)
        )
        part.wait_send()
        part.wait_recv()

    @pl.when(away)
    def _():
        whole = remote(sp_ref, sa_ref, in_send, in_recv, (i, j))
        whole.wait_send()
        whole.wait_recv()

    prepare_sources(sa_ref, w_ref, ph_ref, freq)
    pl.semaphore_wait(ready, N_RCV - 1)

    first = lax.div(me, 16) + 1

    def tile(n):
        return lax.rem(first + n + n_tiles, n_tiles)

    def write(n, sums):
        t = tile(n)
        ms_ref[pl.ds(t * 16, 16)] = message(sums, ph_ref[t], turn_ref)

    def send_out(n, start):
        for d in range(start, 16):
            row = tile(n) * 16 + lax.rem(me + d, 16)
            dest = (lax.div(row, N_RCV), lax.rem(row, N_RCV))
            remote(ms_ref.at[row], so_ref.at[me], out_send, out_recv, dest).start()

    def slants(n):
        phase = ph_ref[tile(n)]
        cos_b = phase[:16].astype(bf)
        sin_b = phase[16:].astype(bf)
        es0 = jnp.concatenate([cos_b, -sin_b], axis=0)
        es1 = jnp.concatenate([sin_b, cos_b], axis=0)
        return es0, es1

    def step(n, carry):
        @pl.when(n >= 2)
        def _():
            send_out(n - 2, 0)

        weights = w_ref[tile(n)]
        old = slants(n - 1)
        new = slants(n)
        cross_chunk(left_ref, weights, g0_ref, 0)
        sums = sums_ref[...] + slant_chunk(er_ref, *old, g3_ref, acc_ref, 3)
        write(n - 1, sums)
        cross_chunk(left_ref, weights, g1_ref, 1)
        sums = slant_chunk(er_ref, *new, g0_ref, acc_ref, 0)
        cross_chunk(left_ref, weights, g2_ref, 2)
        sums = sums + slant_chunk(er_ref, *new, g1_ref, acc_ref, 1)
        cross_chunk(left_ref, weights, g3_ref, 3)
        sums_ref[...] = sums + slant_chunk(er_ref, *new, g2_ref, acc_ref, 2)
        return carry

    lax.fori_loop(0, n_tiles, step, 0)
    last = slants(n_tiles - 1)
    sums = sums_ref[...] + slant_chunk(er_ref, *last, g3_ref, acc_ref, 3)
    write(n_tiles - 1, sums)
    send_out(n_tiles - 2, 0)
    factor = 0.5 / math.sqrt(N_S)
    acc_re, acc_im = acc_ref[:16], acc_ref[16:]
    out_re = (acc_re * cos_r - acc_im * sin_r) * factor
    out_im = (acc_re * sin_r + acc_im * cos_r) * factor
    both = jnp.concatenate([out_re, out_im], axis=0).astype(bf)
    for q in range(N_RCV):
        mr_ref[q] = both[:, q * RB:(q + 1) * RB]
    out_local = pltpu.make_async_copy(ms_ref.at[me], so_ref.at[me], out_keep)
    out_local.start()
    send_out(n_tiles - 1, 1)
    rout_local = pltpu.make_async_copy(mr_ref.at[j], ro_ref.at[j], rout_keep)
    rout_local.start()
    for d in range(1, N_RCV):
        peer = lax.rem(j + d, N_RCV)
        remote(mr_ref.at[peer], ro_ref.at[j], rout_send, rout_recv, (i, peer)).start()
    out_local.wait()
    rout_local.wait()
    rout_rest = remote(
        mr_ref.at[pl.ds(0, N_RCV - 1)], ro_ref.at[pl.ds(0, N_RCV - 1)], rout_send, rout_recv, (i, j)
    )
    rout_rest.wait_send()
    rout_rest.wait_recv()
    out_rest = remote(
        ms_ref.at[pl.ds(0, N_DEV - 1)], so_ref.at[pl.ds(0, N_DEV - 1)], out_send, out_recv, (i, j)
    )
    out_rest.wait_send()
    out_rest.wait_recv()


def panels(src_rows, rcv_rows, lag_table, pos):
    bf = jnp.bfloat16
    f32 = jnp.float32
    msg_s = (N_DEV, 4, 128)
    msg_r = (N_RCV, 2 * N_SLOW, RB)
    vmem = pl.BlockSpec(memory_space=pltpu.VMEM)
    return pl.pallas_call(
        panels_kernel,
        out_shape=(jax.ShapeDtypeStruct(msg_s, bf), jax.ShapeDtypeStruct(msg_r, bf)),
        in_specs=[vmem] * 4,
        out_specs=(vmem,) * 2,
        scratch_shapes=[
            pltpu.VMEM((SB, 24, 128), bf),
            pltpu.VMEM((N_RCV, 48, RB), bf),
            pltpu.VMEM((SB, 24, 128), bf),
            pltpu.VMEM((N_RCV, 48, RB), bf),
            pltpu.VMEM(msg_s, bf),
            pltpu.VMEM(msg_r, bf),
            pltpu.VMEM((N_R // 16, 4, 16, 32), bf),
            pltpu.VMEM((4, 2 * N_SLOW, 2 * RB), bf),
            pltpu.VMEM((N_S // TILE, 32, TILE), bf),
            pltpu.VMEM((N_S // TILE, 2 * N_SLOW, TILE), f32),
            pltpu.VMEM((2 * RB, TILE), bf),
            pltpu.VMEM((2 * RB, TILE), bf),
            pltpu.VMEM((2 * RB, TILE), bf),
            pltpu.VMEM((2 * RB, TILE), bf),
            pltpu.VMEM((2 * N_SLOW, TILE), f32),
            pltpu.VMEM((2 * N_SLOW, N_R), f32),
            pltpu.VMEM((16, 16, 128), f32),
        ] + [pltpu.SemaphoreType.DMA] * 12 + [pltpu.SemaphoreType.REGULAR],
        compiler_params=pltpu.CompilerParams(has_side_effects=True, collective_id=1),
        name="panels",
    )(src_rows, rcv_rows, lag_table, pos)


def arrange_kernel(m_ref, o_ref):
    q = lax.broadcasted_iota(jnp.int32, (512, 128), 0)
    k = lax.broadcasted_iota(jnp.int32, (512, 128), 1)
    p, c, s = q // 32, (q // 16) & 1, q & 15
    lane = (s // 4) * 32 + c * 16 + p
    total = jnp.zeros((512, N_FREQ), jnp.float32)
    nt = (((1,), (1,)), ((), ()))
    for row in range(4):
        pick = jnp.where((k == lane) & ((s & 3) == row), 1.0, 0.0).astype(jnp.bfloat16)
        total = total + lax.dot_general(
            pick, m_ref[:, row, :], nt, preferred_element_type=jnp.float32
        )
    o_ref[...] = total


def arrange(msg):
    return pl.pallas_call(
        arrange_kernel,
        out_shape=jax.ShapeDtypeStruct((512, N_FREQ), jnp.float32),
        name="arrange",
    )(msg)


def per_device(src_spec, rcv_spec, lag_table, src_pos, rcv_pos):
    pos = jnp.concatenate([rcv_pos, src_pos])[None, :]
    src_rows = jnp.transpose(src_spec, (2, 1, 0, 3)).reshape(SB, 16, 128)
    rcv_rows = jnp.transpose(rcv_spec, (2, 0, 1, 3)).reshape(N_RCV, 32, RB)
    src_got, rcv_got = panels(src_rows, rcv_rows, lag_table, pos)
    panel_src = arrange(src_got).reshape(N_SLOW, 2, 16, N_FREQ)
    rcv_got = rcv_got.reshape(N_RCV, 2, N_SLOW, RB)
    panel_rcv = jnp.transpose(rcv_got, (2, 1, 0, 3)).astype(jnp.float32)
    return (panel_src, panel_rcv)


def solution(mesh):
    placed = (P(None, None, "rcv", "src"), P(None, None, "src", "rcv"), P(), P("src"), P("rcv"))
    return jax.shard_map(
        per_device,
        mesh=mesh,
        in_specs=placed,
        out_specs=(P(None, None, ("src", "rcv"), None), P(None, None, "src", "rcv")),
        check_vma=False,
    )
```
